32 devices in a mesh: branch: 8 (over y, x, core), fsdp: 4 (over z).
Axes of the slice: x: 2, y: 2, z: 4, core: 2. Of those that a mesh axis runs over, the one named last changes fastest.
Arguments:
- activations: bfloat16 [8, 128, 192], P('branch', 'fsdp'), may hold values from -16 to 16
- weights: bfloat16 [8, 192, 29568], P('branch', None, 'fsdp'), may hold values from -6 to 6
- output_grads: bfloat16 [8, 128, 29568], P('branch', None, 'fsdp'), may hold values from -16 to 16
Outputs:
- merged: bfloat16 [192, 29568], P(None, 'fsdp')
- mean_fisher: float32 [192, 29568], P(None, 'fsdp')
The draws below stay inside these ranges and needn't reach their ends.
All inputs are finite; a program needn't handle non-finite values.
Results may differ from the reference program's by a relative error of at most 0.0038.
Values may be sent and summed in bfloat16 or wider, within the bound.
No kernel may reach another device: no remote copies, remote signals or barrier semaphores. Data moves between devices by JAX's collectives and lax.ppermute only.
A program may use at most 64 MiB of HBM per device.

```python
import math
import jax
import jax.numpy as jnp
from jax import lax

FF = 29568
ROWS = 192
TOKENS = 128
BRANCHES = 8


def scaled_field(key, width):
    keys = jax.random.split(key, 3)
    groups = 8
    base = jax.random.normal(keys[0], (BRANCHES, TOKENS, width), jnp.float32)
    base = jnp.clip(base, -4.0, 4.0)
    token_scale = jnp.exp(jax.random.uniform(keys[1], (BRANCHES, TOKENS, 1), jnp.float32, math.log(0.2), math.log(2.0)))
    column_scale = jnp.exp(jax.random.uniform(keys[2], (BRANCHES, groups, 1, width), jnp.float32, math.log(0.05), math.log(2.0)))
    grouped = (base * token_scale).reshape(BRANCHES, groups, TOKENS // groups, width) * column_scale
    return grouped.reshape(BRANCHES, TOKENS, width).astype(jnp.bfloat16)


def draw_activations(key, part):
    return scaled_field(jax.random.fold_in(key, 11), ROWS)


def draw_output_grads(key, part):
    return scaled_field(jax.random.fold_in(key, 23), FF)


def block_scale(key, shape, pieces, low, top_value):
    def one(dim, blocks):
        heights = jax.random.uniform(jax.random.fold_in(jax.random.fold_in(key, 6), dim), (blocks,), jnp.float32, low / len(pieces), top_value / len(pieces))
        return jnp.repeat(jnp.exp(heights), shape[dim] // blocks).reshape((-1,) + (1,) * (len(shape) - dim - 1))

    loudness = one(*pieces[0])
    for cut in pieces[1:]:
        loudness = loudness * one(*cut)
    return loudness


def centred(key, shape, scale, bound, pieces=(), kind=jnp.bfloat16):
    level = block_scale(key, shape, pieces, -0.22, 0.18) if pieces else 1.0
    values = jax.random.normal(key, shape, jnp.float32) * scale * level
    return jnp.minimum(jnp.maximum(values, -bound), bound).astype(kind)


def setup_inputs(seed: int = 0) -> dict:
    streams_of = jax.random.split(jax.random.key(seed), 4)
    return {
        "activations": draw_activations(jax.random.fold_in(streams_of[3], 71), 0),
        "weights": centred(streams_of[1], (BRANCHES, ROWS, FF), 1.0, 6.0, ((0, 8), (2, 4))),
        "output_grads": draw_output_grads(jax.random.fold_in(streams_of[3], 71), 0),
    }


def branch_fisher(act_branch, grad_branch):
    act_f = act_branch.astype(jnp.float32)
    act_sq = (act_f * act_f).astype(jnp.bfloat16)
    grad_f = grad_branch.astype(jnp.float32)
    grad_sq = (grad_f * grad_f).astype(jnp.bfloat16)
    fisher = lax.dot_general(act_sq, grad_sq, (((0,), (0,)), ((), ())), preferred_element_type=jnp.float32)
    return fisher / TOKENS


def reference(activations, weights, output_grads):
    def step(carry, items):
        act_branch, w_branch, grad_branch = items
        fisher = branch_fisher(act_branch, grad_branch)
        return (carry[0] + fisher * w_branch.astype(jnp.float32), carry[1] + fisher), None

    start = (jnp.zeros((ROWS, FF), jnp.float32), jnp.zeros((ROWS, FF), jnp.float32))
    totals, unused = lax.scan(step, start, (activations, weights, output_grads))
    total_weighted, total_fisher = totals
    merged = (total_weighted / (total_fisher + 1e-6)).astype(jnp.bfloat16)
    return merged, total_fisher / BRANCHES
```

```python
import functools

import jax
import jax.numpy as jnp
from jax import lax
from jax.experimental import pallas as pl
from jax.experimental.pallas import tpu as pltpu
from jax.sharding import PartitionSpec as P

BF16 = jnp.bfloat16
F32 = jnp.float32
LANES = 128

CORE, OTHER, Q_OWN, Q_X, Q_Y, Q_D, TOK = range(7)
TO_CORE, TO_X, TO_Y = 1, 2, 4


def call(kernel, scalars, arrays, in_specs, outs, out_specs, grid=(1,), scratch=(), aliases=None, flops=0):
    moved = sum(a.size * a.dtype.itemsize for a in jax.tree.leaves((arrays, outs)))
    return pl.pallas_call(
        kernel,
        out_shape=outs,
        grid_spec=pltpu.PrefetchScalarGridSpec(
            num_scalar_prefetch=1, grid=grid, in_specs=in_specs, out_specs=out_specs, scratch_shapes=list(scratch)
        ),
        input_output_aliases=aliases or {},
        cost_estimate=pl.CostEstimate(flops=flops, bytes_accessed=moved, transcendentals=0),
        compiler_params=pltpu.CompilerParams(vmem_limit_bytes=56 * 2**20),
    )(scalars, *arrays)


def sds(shape, dtype):
    return jax.ShapeDtypeStruct(shape, dtype)


def fixed(shape, *at):
    at = at or (0,) * len(shape)
    return pl.BlockSpec(shape, lambda *_: at)


def pieces(width, step=512):
    return [(c, min(step, width - c)) for c in range(0, width, step)]


def split_kernel(s, w, g, w_out, g_out):
    w_out[...] = w[...]
    g_out[...] = g[...]


def products(act_t, rows, gsq, w_mine, w_theirs, inv_tokens, store):
    lhs = [act_t[b, rows, :] for b in range(2)]
    dims = (((1,), (1,)), ((), ()))
    for c, n in pieces(gsq.shape[1]):
        f = [
            lax.dot_general(lhs[b], gsq[b, c : c + n, :], dims, preferred_element_type=F32) * inv_tokens
            for b in range(2)
        ]
        mine, theirs = (w[:, c : c + n].astype(F32) for w in (w_mine, w_theirs))
        store(c, n, f[0] * mine + f[1] * theirs, f[0] + f[1])


def first_kernel(n_acts, quarter, inv_tokens, s, *refs):
    acts = refs[:n_acts]
    g_mine, g_theirs, w_mine, w_theirs, w_out, f_out, act_t, gsq, gathered = refs[n_acts:]
    per = acts[0].shape[1]
    for k, act in enumerate(acts):
        at = pl.ds(pl.multiple_of(s[TOK + k] * per, per), per)
        for b in range(2):
            a = act[b].astype(F32)
            gathered[b, at, :] = (a * a).astype(BF16).astype(F32)
    for b in range(2):
        act_t[b] = gathered[b].T.astype(BF16)
    for b, g in enumerate((g_mine, g_theirs)):
        for c, n in pieces(g.shape[0]):
            v = g[c : c + n, :].astype(F32)
            gsq[b, c : c + n, :] = (v * v).astype(BF16)

    def store(c, n, weighted, fisher):
        w_out[:, c : c + n] = weighted.astype(BF16)
        f_out[:, c : c + n] = fisher.astype(BF16)

    quart = w_mine.shape[0]
    rows = pl.ds(pl.multiple_of(s[quarter] * quart, quart), quart)
    products(act_t, rows, gsq, w_mine, w_theirs, inv_tokens, store)


def side_kernel(inv_tokens, s, act_t, gsq, w_mine, w_theirs, wx_out, fx_out, wy_out, fy_out):
    quart = w_mine.shape[0]

    def step(quarter, w_out, f_out):
        def store(c, n, weighted, fisher):
            w_out[:, c : c + n] = weighted.astype(w_out.dtype)
            f_out[:, c : c + n] = fisher.astype(f_out.dtype)

        rows = pl.ds(pl.multiple_of(s[quarter] * quart, quart), quart)
        products(act_t, rows, gsq, w_mine, w_theirs, inv_tokens, store)

    @pl.when(pl.program_id(0) == 0)
    def _():
        step(Q_X, wx_out, fx_out)

    @pl.when(pl.program_id(0) == 1)
    def _():
        step(Q_Y, wy_out, fy_out)


def own_kernel(inv_tokens, s, act_t, gsq, w_mine, w_theirs, w_out, f_out):
    quart = w_mine.shape[0]

    def store(c, n, weighted, fisher):
        w_out[:, c : c + n] = weighted
        f_out[:, c : c + n] = fisher

    rows = pl.ds(pl.multiple_of(s[Q_OWN] * quart, quart), quart)
    products(act_t, rows, gsq, w_mine, w_theirs, inv_tokens, store)


def relay_kernel(s, fx, wy, w_in, f_in, xa, xb, ya, yb):
    half = xa.shape[0]
    for c, n in pieces(fx.shape[1]):
        cols = slice(c, c + n)
        x = (fx[:, cols] + f_in[:, cols].astype(F32)).astype(BF16)
        y = (wy[:, cols] + w_in[:, cols].astype(F32)).astype(BF16)
        xa[:, cols], xb[:, cols] = x[:half], x[half:]
        ya[:, cols], yb[:, cols] = y[:half], y[half:]


def total_kernel(s, w0, f0, wx, fy, fx, wy, w_out, f_out):
    for c, n in pieces(w0.shape[1]):
        cols = slice(c, c + n)
        w_out[:, cols] = w0[:, cols] + wx[:, cols].astype(F32) + wy[:, cols].astype(F32)
        f_out[:, cols] = f0[:, cols] + fy[:, cols].astype(F32) + fx[:, cols].astype(F32)


def finish_kernel(inv_branches, s, w0, f0, wx, fy, fx, wy, out):
    for c, n in pieces(w0.shape[1]):
        cols = slice(c, c + n)
        weighted = w0[:, cols] + wx[:, cols].astype(F32) + wy[:, cols].astype(F32)
        fisher = f0[:, cols] + fy[:, cols].astype(F32) + fx[:, cols].astype(F32)
        out[0, :, cols] = (weighted / (fisher + 1e-6)).astype(BF16)
        out[1, :, cols] = (fisher * inv_branches).astype(BF16)


def place_kernel(groups, s, *refs):
    merged_out, mean_out = refs[-2:]
    for step, group in enumerate(groups):

        @pl.when(pl.program_id(0) == step)
        def _(group=group):
            row = 0
            for merged, merged_at, mean, mean_at in group:
                m, f = refs[merged], refs[mean]
                n = m.shape[-2]
                for c, w in pieces(m.shape[-1], 1024):
                    cols = slice(c, c + w)
                    mv = m[:, cols] if merged_at is None else m[merged_at, :, cols]
                    fv = f[:, cols] if mean_at is None else f[mean_at, :, cols]
                    merged_out[row : row + n, cols] = mv
                    mean_out[row : row + n, cols] = fv.astype(F32)
                row += n


def on_device(activations, weights, output_grads):
    branches = lax.axis_size("branch")
    shards = lax.axis_size("fsdp")
    rows, cols = weights.shape[1:]
    tokens = output_grads.shape[1]
    width = pl.cdiv(cols, 2 * LANES) * LANES
    quart = rows // 4
    half = quart // 2
    inv_tokens = 1.0 / tokens

    def flip(x, bit):
        return lax.ppermute(x, "branch", [(i, i ^ bit) for i in range(branches)])

    me = lax.axis_index("branch")
    z = lax.axis_index("fsdp")
    core, xi, yi = me & 1, (me >> 1) & 1, (me >> 2) & 1
    quarters = [2 * xi + yi, 2 * (1 - xi) + yi, 2 * xi + 1 - yi, 2 * (1 - xi) + 1 - yi]
    hops = list(range(1, shards))
    s = jnp.stack([core, 1 - core, *quarters, z, *[z ^ k for k in hops]]).astype(jnp.int32)

    w = weights[0]
    g = output_grads[0].T
    run = functools.partial(call, scalars=s)

    pair = jnp.concatenate([activations, flip(activations, TO_CORE)], axis=0)
    acts = [pair] + [lax.ppermute(pair, "fsdp", [(i, i ^ k) for i in range(shards)]) for k in hops]

    steps = 4
    wr, gr = rows // steps, width // steps
    w_send, g_send = run(
        split_kernel,
        arrays=[w, g],
        in_specs=[
            pl.BlockSpec((wr, width), lambda i, s: (i, s[OTHER])),
            pl.BlockSpec((gr, tokens), lambda i, s: (s[OTHER] * steps + i, 0)),
        ],
        outs=[sds((rows, width), BF16), sds((width, tokens), BF16)],
        out_specs=[pl.BlockSpec((wr, width), lambda i, s: (i, 0)), pl.BlockSpec((gr, tokens), lambda i, s: (i, 0))],
        grid=(steps,),
    )
    g_got = flip(g_send, TO_CORE)
    w_got = flip(w_send, TO_CORE)

    flops = 2 * 2 * quart * width * tokens
    quarter_f32, quarter_b16 = sds((quart, width), F32), sds((quart, width), BF16)
    w_dd, f_dd, act_t, gsq = run(
        functools.partial(first_kernel, len(acts), Q_D, inv_tokens),
        arrays=[*acts, g, g_got, w, w_got],
        in_specs=[fixed(pair.shape)] * len(acts)
        + [
            pl.BlockSpec((width, tokens), lambda i, s: (s[CORE], 0)),
            fixed((width, tokens)),
            pl.BlockSpec((quart, width), lambda i, s: (s[Q_D], s[CORE])),
            pl.BlockSpec((quart, width), lambda i, s: (s[Q_D], 0)),
        ],
        outs=[quarter_b16, quarter_b16, sds((2, rows, tokens), BF16), sds((2, width, tokens), BF16)],
        out_specs=[fixed((quart, width))] * 2 + [fixed((2, rows, tokens)), fixed((2, width, tokens))],
        scratch=[pltpu.VMEM((2, tokens, rows), F32)],
        flops=flops,
    )
    x1 = flip(w_dd, TO_X)
    y1 = flip(f_dd, TO_Y)

    square_specs = [fixed(act_t.shape), fixed(gsq.shape)]
    x2, fx, wy, y2 = run(
        functools.partial(side_kernel, inv_tokens),
        arrays=[act_t, gsq, w, w_got],
        in_specs=square_specs
        + [
            pl.BlockSpec((quart, width), lambda i, s: (s[Q_X + i], s[CORE])),
            pl.BlockSpec((quart, width), lambda i, s: (s[Q_X + i], 0)),
        ],
        outs=[quarter_b16, quarter_f32, quarter_f32, quarter_b16],
        out_specs=[fixed((quart, width))] * 4,
        grid=(2,),
        flops=2 * flops,
    )
    x2 = flip(x2, TO_X)
    y2 = flip(y2, TO_Y)

    w0, f0 = run(
        functools.partial(own_kernel, inv_tokens),
        arrays=[act_t, gsq, w, w_got],
        in_specs=square_specs
        + [
            pl.BlockSpec((quart, width), lambda i, s: (s[Q_OWN], s[CORE])),
            pl.BlockSpec((quart, width), lambda i, s: (s[Q_OWN], 0)),
        ],
        outs=[quarter_f32, quarter_f32],
        out_specs=[fixed((quart, width))] * 2,
        flops=flops,
    )

    half_b16 = sds((half, width), BF16)
    xa, xb, ya, yb = run(
        relay_kernel,
        arrays=[fx, wy, x1, y1],
        in_specs=[fixed((quart, width))] * 4,
        outs=[half_b16] * 4,
        out_specs=[fixed((half, width))] * 4,
    )
    own, from_x, from_y = [], [], []
    for h, (x3, y3) in enumerate(((flip(xa, TO_X), flip(ya, TO_Y)), (flip(xb, TO_X), flip(yb, TO_Y)))):
        terms = [w0, f0, x2, y2, x3, y3]
        specs = [fixed((half, width), h, 0)] * 4 + [fixed((half, width))] * 2
        if branches == 8:
            done = run(
                functools.partial(finish_kernel, 1.0 / branches),
                arrays=terms,
                in_specs=specs,
                outs=sds((2, half, width), BF16),
                out_specs=fixed((2, half, width)),
            )
        else:
            totals = run(
                total_kernel, arrays=terms, in_specs=specs, outs=[sds((half, width), F32)] * 2, out_specs=[fixed((half, width))] * 2
            )
            groups = [list(range(i, branches, 8)) for i in range(8)]
            weighted, fisher = lax.psum(tuple(totals), "branch", axis_index_groups=groups)
            done = jnp.stack([(weighted / (fisher + 1e-6)).astype(BF16), (fisher / branches).astype(BF16)])
        own.append(done)
        from_x.append(flip(done, TO_X))
        from_y.append(flip(done, TO_Y))
    merged_d = [flip(y[0], TO_X) for y in from_y]
    mean_d = [flip(x[1], TO_Y) for x in from_x]

    def place(mine, groups, quarters, into):
        theirs = [flip(p, TO_CORE) for p in mine]
        n = len(mine)
        both = groups + [[(a + n, b, c + n, d) for a, b, c, d in group] for group in groups]
        per = len(groups)

        def at(i, s):
            quarter = s[quarters[0]] if per == 1 else s[quarters[0] + i % per]
            return quarter, jnp.where(i < per, s[CORE], s[OTHER])

        block = pl.BlockSpec((quart, width), at)
        arrays = [*mine, *theirs, *into]
        return run(
            functools.partial(place_kernel, both),
            arrays=arrays,
            in_specs=[fixed(p.shape) for p in [*mine, *theirs]] + [pl.BlockSpec(memory_space=pl.ANY)] * len(into),
            outs=[sds((rows, cols), BF16), sds((rows, cols), F32)],
            out_specs=[block, block],
            grid=(2 * per,),
            aliases={1 + 2 * n + k: k for k in range(len(into))},
        )

    out = place(own, [[(0, 0, 0, 1), (1, 0, 1, 1)]], [Q_OWN], ())
    out = place([*from_x, *from_y], [[(0, 0, 0, 1), (1, 0, 1, 1)], [(2, 0, 2, 1), (3, 0, 3, 1)]], [Q_X], out)
    out = place([*merged_d, *mean_d], [[(0, None, 2, None), (1, None, 3, None)]], [Q_D], out)
    return tuple(out)


def solution(mesh):
    placed = (P("branch", "fsdp", None), P("branch", None, "fsdp"), P("branch", None, "fsdp"))
    return jax.shard_map(
        on_device,
        mesh=mesh,
        in_specs=placed,
        out_specs=(P(None, "fsdp"), P(None, "fsdp")),
        check_vma=False,
    )
```
